128 devices in a mesh: walk: 8 (over x, core), blk: 16 (over y, z).
Axes of the slice: x: 4, y: 4, z: 4, core: 2. Of those that a mesh axis runs over, the one named last changes fastest.
Arguments:
- derivs: bfloat16 [1536, 409600], P('walk', 'blk'), may hold values from -0.5 to 1.5
- energy_grads: bfloat16 [1536, 409600], P('walk', 'blk'), may hold values from -0.5 to 1.5
- local_energy: float32 [1536], P('walk'), may hold values from -6 to 6
- directions: bfloat16 [512, 25600], P('blk'), may hold values from -0.0390625 to 0.0390625
- widths: int32 [16], P('blk'), may hold values from 6400 to 25600, as said below
- live_rows: int32 [8], P('walk'), may hold values from 96 to 192, as said below
Outputs:
- hamiltonian: float32 [512, 512], P('blk', 'walk')
- correlation: float32 [512, 512], P('blk', 'walk')
The draws below stay inside these ranges and needn't reach their ends.
Inputs may be any that keep to these rules, and one draw needn't show every extreme that they name: `widths`: each block uses between a quarter of its 25600 slots and all of them; some block uses all 25600. `live_rows`: each group has at least half of its 192 slots live; some group has all 192 live.
All inputs are finite; a program needn't handle non-finite values.
Results may differ from the reference program's by a relative error of at most 0.0041.
Values may be sent and summed in bfloat16 or wider, within the bound.
A program may use at most 64 MiB of HBM per device.

```python
import jax
import jax.numpy as jnp

PMAX = 25600
DIRS = 32
ROWS_DEV = 192
BLOCKS = 16
WALK_DEVS = 8
WALKERS = 1536
PARAMS = 409600
RANK = 512


def draw_widths(key, part):
    values = jax.random.randint(jax.random.fold_in(key, 11), (BLOCKS,), PMAX // 4, PMAX + 1)
    chosen = jax.random.randint(jax.random.fold_in(key, 12), (), 0, BLOCKS)
    return values.at[chosen].set(PMAX).astype(jnp.int32)


def draw_live_rows(key, part):
    values = jax.random.randint(jax.random.fold_in(key, 21), (WALK_DEVS,), ROWS_DEV // 2, ROWS_DEV + 1)
    chosen = jax.random.randint(jax.random.fold_in(key, 22), (), 0, WALK_DEVS)
    return values.at[chosen].set(ROWS_DEV).astype(jnp.int32)


def block_levels(stream_key, dims, split, low, high):
    def one(position, parts):
        draws = jax.random.uniform(jax.random.fold_in(jax.random.fold_in(stream_key, 6), position), (parts,), jnp.float32, low / len(split), high / len(split))
        return jnp.repeat(jnp.exp(draws), dims[position] // parts).reshape((-1,) + (1,) * (len(dims) - position - 1))

    loudness = one(*split[0])
    for cut in split[1:]:
        loudness = loudness * one(*cut)
    return loudness


def gaussian(rng, extent, deviation, reach, split=(), kind=jnp.bfloat16):
    array = deviation * jax.random.normal(rng, extent, jnp.float32)
    if split:
        array = array * block_levels(rng, extent, split, -0.22, 0.18)
    return jnp.clip(array, -reach, reach).astype(kind)


def setup_inputs(seed: int = 0) -> dict:
    streams_of = jax.random.split(jax.random.key(seed), 7)
    return {
        "derivs": jnp.clip(-0.5 + 2.0 * jax.random.uniform(streams_of[0], (WALKERS, PARAMS), jnp.float32) ** block_levels(streams_of[0], (WALKERS, PARAMS), ((0, 8), (1, 16)), -0.2, 0.2), -0.5, 1.5).astype(jnp.bfloat16),
        "energy_grads": jnp.clip(-0.5 + 2.0 * jax.random.uniform(streams_of[1], (WALKERS, PARAMS), jnp.float32) ** block_levels(streams_of[1], (WALKERS, PARAMS), ((0, 8), (1, 16)), -0.2, 0.2), -0.5, 1.5).astype(jnp.bfloat16),
        "local_energy": gaussian(streams_of[2], (WALKERS,), 1.0, 6.0, ((0, 8),), jnp.float32),
        "directions": gaussian(streams_of[3], (RANK, PMAX), PMAX ** -0.5, 0.0390625, ((0, 16),)),
        "widths": draw_widths(jax.random.fold_in(streams_of[6], 71), 0),
        "live_rows": draw_live_rows(jax.random.fold_in(streams_of[6], 71), 0),
    }


def reference(derivs, energy_grads, local_energy, directions, widths, live_rows):
    column = jnp.arange(PMAX, dtype=jnp.int32)
    projs = []
    projqs = []
    for block in range(BLOCKS):
        keep = (column < widths[block])[None, :]
        dirs = directions[block * DIRS:(block + 1) * DIRS]
        rows = jnp.where(keep, derivs[:, block * PMAX:(block + 1) * PMAX], jnp.zeros((), jnp.bfloat16))
        grads = jnp.where(keep, energy_grads[:, block * PMAX:(block + 1) * PMAX], jnp.zeros((), jnp.bfloat16))
        projs.append(jnp.dot(rows, dirs.T, preferred_element_type=jnp.float32))
        projqs.append(jnp.dot(grads, dirs.T, preferred_element_type=jnp.float32))
    proj = jnp.concatenate(projs, axis=1)
    projq = jnp.concatenate(projqs, axis=1)
    slot = jnp.arange(ROWS_DEV, dtype=jnp.int32)
    live = (slot[None, :] < live_rows[:, None]).reshape(WALKERS).astype(jnp.float32)[:, None]
    count = jnp.sum(live)
    pbar = jnp.sum(proj * live, axis=0) / count
    qbar = jnp.sum(projq * live, axis=0) / count
    centred = proj - pbar
    pc = (live * centred).astype(jnp.bfloat16)
    hc = (live * (local_energy[:, None] * centred + projq - qbar)).astype(jnp.bfloat16)
    correlation = jnp.dot(pc.T, pc, preferred_element_type=jnp.float32) / count
    hamiltonian = jnp.dot(pc.T, hc, preferred_element_type=jnp.float32) / count
    return hamiltonian, correlation
```

```python
import functools

import jax
import jax.numpy as jnp
from jax import lax
from jax.experimental import pallas as pl
from jax.experimental.pallas import tpu as pltpu
from jax.sharding import PartitionSpec as P

MESH = pl.DeviceIdType.MESH
F32 = jnp.float32
BF16 = jnp.bfloat16
CHUNK = 64
LANES = 128
SPLIT = 2
AHEAD = 3
NT = (((1,), (1,)), ((), ()))
TN = (((0,), (0,)), ((), ()))


def exact_dot(a, b, dims):
    return lax.dot_general(
        a, b, dims, precision=lax.Precision.HIGHEST, preferred_element_type=F32
    )


def pencil_kernel(
    nw, nb, d_hbm, e_hbm, v_hbm, en_ref, wid_ref, live_ref, o_ref,
    dv, ev, vv, panel, tail, lhs, shift, msg, got,
    dsem, esem, vsem, csend, crecv, asend, arecv, bsend, brecv, msend, mrecv,
):
    w = lax.axis_index("walk")
    b = lax.axis_index("blk")
    rows, cols = d_hbm.shape
    dirs = v_hbm.shape[0]
    width = cols // SPLIT
    chunks = rows // CHUNK
    pieces = [(c, k) for c in range(chunks) for k in range(SPLIT)]

    def dir_copy(k):
        part = (slice(None), pl.ds(k * width, width))
        return pltpu.make_async_copy(v_hbm.at[part], vv.at[part], vsem.at[k])

    def piece_copies(i):
        c, k = pieces[i]
        part = (pl.ds(c * CHUNK, CHUNK), pl.ds(k * width, width))
        return (
            pltpu.make_async_copy(d_hbm.at[part], dv.at[part], dsem.at[i]),
            pltpu.make_async_copy(e_hbm.at[part], ev.at[part], esem.at[i]),
        )

    def start_piece(i):
        if i < SPLIT:
            dir_copy(i).start()
        for copy in piece_copies(i):
            copy.start()

    for i in range(AHEAD):
        start_piece(i)

    walk_peers = [lax.rem(w + r, nw) for r in range(1, nw)]
    blk_peers = [lax.rem(b + r, nb) for r in range(1, nb)]
    barrier = pltpu.get_barrier_semaphore()
    for peer in walk_peers:
        pl.semaphore_signal(barrier, inc=1, device_id=(peer, b), device_id_type=MESH)
    for peer in blk_peers:
        pl.semaphore_signal(barrier, inc=1, device_id=(w, peer), device_id_type=MESH)

    lane = lax.broadcasted_iota(jnp.int32, (1, LANES), 1)
    low = lane < CHUNK
    used = wid_ref[0]
    live_rows = live_ref[0]

    def project(c):
        total = None
        for k in range(SPLIT):
            i = c * SPLIT + k
            span = pl.ds(k * width, width)
            if c == 0:
                dir_copy(k).wait()
                column = lax.broadcasted_iota(jnp.int32, (dirs, width), 1) + k * width
                vv[:, span] = jnp.where(
                    column < used, vv[:, span].astype(F32), 0.0
                ).astype(BF16)
            for copy in piece_copies(i):
                copy.wait()
            if i + AHEAD < len(pieces):
                start_piece(i + AHEAD)
            rs = pl.ds(c * CHUNK, CHUNK)
            weights = vv[:, span]
            part = jnp.concatenate(
                [
                    lax.dot_general(weights, dv[rs, span], NT, preferred_element_type=F32),
                    lax.dot_general(weights, ev[rs, span], NT, preferred_element_type=F32),
                ],
                axis=1,
            )
            total = part if total is None else total + part
        return total

    row8 = lax.broadcasted_iota(jnp.int32, (8, LANES), 0)
    lane8 = lax.broadcasted_iota(jnp.int32, (8, LANES), 1)
    first_low = jnp.where((row8 == 0) & (lane8 < CHUNK), 1.0, 0.0)
    first_high = jnp.where((row8 == 0) & (lane8 >= CHUNK), 1.0, 0.0)
    halves = first_low + jnp.where((row8 == 1) & (lane8 >= CHUNK), 1.0, 0.0)

    def energies(c):
        lo = (c * CHUNK) // LANES * LANES
        if c % 2 == 0 and lo + LANES > rows:
            e = jnp.concatenate(
                [en_ref[:, lo:rows], jnp.zeros((1, LANES - (rows - lo)), F32)], axis=1
            )
        else:
            e = en_ref[:, lo : lo + LANES]
        if c % 2:
            e = pltpu.roll(e, CHUNK, 1)
        walker = c * CHUNK + lane
        return jnp.where(low & (walker < live_rows), e, 0.0)

    def panels(c, s, common):
        walker = c * CHUNK + jnp.where(low, lane, lane - CHUNK)
        d = jnp.where(walker < live_rows, s - common, 0.0)
        erow = energies(c)
        g = (d + pltpu.roll(d * erow, CHUNK, 1)).astype(BF16)
        own = jnp.where(low, g.astype(F32), 0.0)
        lhs[c] = jnp.concatenate(
            [own, first_low, pltpu.roll(own, CHUNK, 1), first_high], axis=0
        ).astype(BF16)
        probe = jnp.where(row8 == 1, erow, first_low)
        return g, exact_dot(probe, own, NT), erow

    s0 = project(0)
    pl.semaphore_wait(barrier, nw - 1 + nb - 1)

    mean = exact_dot(halves * (1.0 / CHUNK), s0, NT)
    shift[w] = jnp.concatenate([mean, jnp.zeros((8, LANES - dirs), F32)], axis=1)
    for peer in walk_peers:
        pltpu.make_async_remote_copy(
            src_ref=shift.at[w], dst_ref=shift.at[w], send_sem=csend, recv_sem=crecv,
            device_id=(peer, b), device_id_type=MESH,
        ).start()

    s1 = project(1)
    others = pl.ds(0, nw - 1)
    pltpu.make_async_copy(shift.at[others], shift.at[others], crecv).wait()
    common = shift[0]
    for i in range(1, nw):
        common = common + shift[i]
    common = exact_dot(common[:, :dirs] * (1.0 / nw), halves, TN)

    g0, rv0, e0 = panels(0, s0, common)
    g1, rv1, e1 = panels(1, s1, common)
    panel[b, 0] = g0
    panel[b, 1] = g1
    for peer in blk_peers:
        pltpu.make_async_remote_copy(
            src_ref=panel.at[b], dst_ref=panel.at[b], send_sem=asend, recv_sem=arecv,
            device_id=(w, peer), device_id_type=MESH,
        ).start()

    s2 = project(2)
    g2, rv2, e2 = panels(2, s2, common)
    tail[b] = g2
    for peer in blk_peers:
        pltpu.make_async_remote_copy(
            src_ref=tail.at[b], dst_ref=tail.at[b], send_sem=bsend, recv_sem=brecv,
            device_id=(w, peer), device_id_type=MESH,
        ).start()

    rv = rv0 + rv1 + rv2
    esum = jnp.sum(e0 + e1 + e2, axis=1, keepdims=True)
    rv = jnp.concatenate([rv, jnp.zeros((8, LANES - dirs), F32)], axis=1)
    small = jnp.where(
        row8 == 1,
        rv[0:1, :],
        jnp.where(
            row8 == 2,
            rv[1:2, :],
            jnp.where(row8 == 3, esum, jnp.where(row8 == 4, live_rows.astype(F32), 0.0)),
        ),
    )

    pair = pl.ds(0, nb - 1)
    pltpu.make_async_copy(panel.at[pair], panel.at[pair], arecv).wait()
    gram = lax.dot_general(
        lhs[0], panel[:, 0].reshape(nb * dirs, LANES), NT, preferred_element_type=F32
    ) + lax.dot_general(
        lhs[1], panel[:, 1].reshape(nb * dirs, LANES), NT, preferred_element_type=F32
    )
    pltpu.make_async_copy(tail.at[pair], tail.at[pair], brecv).wait()
    gram = gram + lax.dot_general(
        lhs[2], tail[...].reshape(nb * dirs, LANES), NT, preferred_element_type=F32
    )
    high = dirs + 8
    extra = jnp.concatenate([jnp.zeros((dirs, LANES), F32), small], axis=0)
    for t in range(nb * dirs // LANES):
        tile = gram[:, t * LANES : (t + 1) * LANES]
        cpart, hpart = tile[:high], tile[high:]
        msg[2 * t] = jnp.where(low, cpart, pltpu.roll(hpart, CHUNK, 1)) + extra
        msg[2 * t + 1] = jnp.where(low, pltpu.roll(cpart, CHUNK, 1), hpart) + extra
    for peer in walk_peers:
        pltpu.make_async_remote_copy(
            src_ref=msg.at[peer], dst_ref=got.at[w], send_sem=msend, recv_sem=mrecv,
            device_id=(peer, b), device_id_type=MESH,
        ).start()
    got[w] = msg[w]

    pltpu.make_async_copy(shift.at[others], shift.at[others], csend).wait()
    pltpu.make_async_copy(panel.at[pair], panel.at[pair], asend).wait()
    pltpu.make_async_copy(tail.at[pair], tail.at[pair], bsend).wait()
    pltpu.make_async_copy(got.at[others], got.at[others], mrecv).wait()

    total = got[0]
    for i in range(1, nw):
        total = total + got[i]
    jsum = total[dirs : dirs + 1]
    isum = total[dirs + 1 : dirs + 2, :dirs]
    usum = total[dirs + 2 : dirs + 3, :dirs]
    esum = total[dirs + 3 : dirs + 4]
    inv = 1.0 / total[dirs + 4 : dirs + 5]
    di = isum * inv[:, :dirs]
    wi = usum - di * esum[:, :dirs]
    dj = jnp.where(low, 0.0, pltpu.roll(jsum * inv, CHUNK, 1))
    left = jnp.where(row8[:, :dirs] == 0, di, jnp.where(row8[:, :dirs] == 1, wi, 0.0))
    right = jnp.where(row8 == 0, jsum, jnp.where(row8 == 1, dj, 0.0))
    o_ref[...] = (total[:dirs] - exact_dot(left, right, TN)) * inv
    pltpu.make_async_copy(got.at[others], got.at[others], msend).wait()


def solution(mesh):
    nw, nb = mesh.shape["walk"], mesh.shape["blk"]

    def per_device(derivs, energy_grads, local_energy, directions, widths, live_rows):
        rows, cols = derivs.shape
        dirs = directions.shape[0]
        chunks = rows // CHUNK
        any_spec = pl.BlockSpec(memory_space=pl.ANY)
        smem_spec = pl.BlockSpec(memory_space=pltpu.SMEM)
        vmem_spec = pl.BlockSpec(memory_space=pltpu.VMEM)
        dma = pltpu.SemaphoreType.DMA
        out = pl.pallas_call(
            functools.partial(pencil_kernel, nw, nb),
            out_shape=jax.ShapeDtypeStruct((dirs, LANES), F32),
            in_specs=[any_spec, any_spec, any_spec, vmem_spec, smem_spec, smem_spec],
            out_specs=vmem_spec,
            scratch_shapes=[
                pltpu.VMEM((rows, cols), BF16),
                pltpu.VMEM((rows, cols), BF16),
                pltpu.VMEM((dirs, cols), BF16),
                pltpu.VMEM((nb, 2, dirs, LANES), BF16),
                pltpu.VMEM((nb, dirs, LANES), BF16),
                pltpu.VMEM((chunks, 2 * (dirs + 8), LANES), BF16),
                pltpu.VMEM((nw, 8, LANES), F32),
                pltpu.VMEM((nw, dirs + 8, LANES), F32),
                pltpu.VMEM((nw, dirs + 8, LANES), F32),
                dma((chunks * SPLIT,)),
                dma((chunks * SPLIT,)),
                dma((SPLIT,)),
            ]
            + [dma(())] * 8,
            compiler_params=pltpu.CompilerParams(
                collective_id=0, has_side_effects=True, vmem_limit_bytes=48 << 20
            ),
            name="pencil",
        )(
            derivs, energy_grads, directions, local_energy.reshape(1, rows), widths, live_rows
        )
        return out[:, CHUNK:], out[:, :CHUNK]

    return jax.shard_map(
        per_device,
        mesh=mesh,
        in_specs=(
            P("walk", "blk"), P("walk", "blk"), P("walk"), P("blk", None), P("blk"), P("walk"),
        ),
        out_specs=(P("blk", "walk"), P("blk", "walk")),
        check_vma=False,
    )
```

```python
import functools

import jax
import jax.numpy as jnp
from jax import lax
from jax.experimental import pallas as pl
from jax.experimental.pallas import tpu as pltpu
from jax.sharding import PartitionSpec as P

MESH = pl.DeviceIdType.MESH
F32 = jnp.float32
BF16 = jnp.bfloat16
CHUNK = 64
LANES = 128
SPLIT = 2
AHEAD = 3
EARLY = 2
NT = (((1,), (1,)), ((), ()))
TN = (((0,), (0,)), ((), ()))


def exact_dot(a, b, dims):
    return lax.dot_general(
        a, b, dims, precision=lax.Precision.HIGHEST, preferred_element_type=F32
    )


def two_terms(x):
    hi = x.astype(BF16).astype(F32)
    return hi, (x - hi).astype(BF16).astype(F32)


def ring_peers(me, count, inner):
    outer = count // inner
    hops = lambda n, size: min(n, size - n)
    steps = [(i, j) for i in range(outer) for j in range(inner) if (i, j) != (0, 0)]
    steps.sort(key=lambda s: -(hops(s[0], outer) + hops(s[1], inner)))
    major, minor = me // inner, lax.rem(me, inner)
    return [
        lax.rem(major + i, outer) * inner + lax.rem(minor + j, inner) for i, j in steps
    ]


def pencil_kernel(
    nw, nb, d_hbm, e_hbm, v_hbm, en_hbm, wid_ref, live_ref, o_ref,
    dv, ev, vv, en_ref, panel, tail, lhs, msg, got, vecs,
    dsem, esem, vsem, ensem, asend, arecv, bsend, brecv, msend, mrecv,
):
    w = lax.axis_index("walk")
    b = lax.axis_index("blk")
    rows, cols = d_hbm.shape
    dirs = v_hbm.shape[0]
    width = cols // SPLIT
    chunks = rows // CHUNK
    pieces = [(c, k) for c in range(chunks) for k in range(SPLIT)]

    def dir_copy(k):
        part = (slice(None), pl.ds(k * width, width))
        return pltpu.make_async_copy(v_hbm.at[part], vv.at[part], vsem.at[k])

    def piece_copies(i):
        c, k = pieces[i]
        part = (pl.ds(c * CHUNK, CHUNK), pl.ds(k * width, width))
        return (
            pltpu.make_async_copy(d_hbm.at[part], dv.at[part], dsem.at[i]),
            pltpu.make_async_copy(e_hbm.at[part], ev.at[part], esem.at[i]),
        )

    def start_piece(i):
        if i < SPLIT:
            dir_copy(i).start()
        for copy in piece_copies(i):
            copy.start()

    en_copy = pltpu.make_async_copy(en_hbm, en_ref, ensem)
    for i in range(AHEAD):
        start_piece(i)
    en_copy.start()

    walk_peers = ring_peers(w, nw, 2)
    blk_peers = ring_peers(b, nb, 4)
    barrier = pltpu.get_barrier_semaphore()
    for peer in blk_peers:
        pl.semaphore_signal(barrier, inc=1, device_id=(w, peer), device_id_type=MESH)
    for peer in walk_peers:
        pl.semaphore_signal(barrier, inc=1, device_id=(peer, b), device_id_type=MESH)

    lane = lax.broadcasted_iota(jnp.int32, (1, LANES), 1)
    low = lane < CHUNK
    used = wid_ref[0]
    live_rows = live_ref[0]

    def project(c):
        total = None
        for k in range(SPLIT):
            i = c * SPLIT + k
            span = pl.ds(k * width, width)
            if c == 0:
                dir_copy(k).wait()
                column = lax.broadcasted_iota(jnp.int32, (dirs, width), 1) + k * width
                vv[:, span] = jnp.where(
                    column < used, vv[:, span].astype(F32), 0.0
                ).astype(BF16)
            for copy in piece_copies(i):
                copy.wait()
            if i + AHEAD < len(pieces):
                start_piece(i + AHEAD)
            rs = pl.ds(c * CHUNK, CHUNK)
            weights = vv[:, span]
            part = jnp.concatenate(
                [
                    lax.dot_general(weights, dv[rs, span], NT, preferred_element_type=F32),
                    lax.dot_general(weights, ev[rs, span], NT, preferred_element_type=F32),
                ],
                axis=1,
            )
            total = part if total is None else total + part
        return total

    row8 = lax.broadcasted_iota(jnp.int32, (8, LANES), 0)
    lane8 = lax.broadcasted_iota(jnp.int32, (8, LANES), 1)

    def mark(row, lo, hi):
        return jnp.where((row8 == row) & (lane8 >= lo) & (lane8 < hi), 1.0, 0.0)

    first_low = mark(0, 0, CHUNK)
    first_high = mark(0, CHUNK, LANES)
    blank = jnp.zeros((dirs, LANES), F32)
    tall = 2 * dirs + 8

    def energies(c):
        lo = (c * CHUNK) // LANES * LANES
        if lo + LANES > rows:
            e = jnp.concatenate(
                [en_ref[:, lo:rows], jnp.zeros((1, LANES - (rows - lo)), F32)], axis=1
            )
        else:
            e = en_ref[:, lo : lo + LANES]
        if c % 2:
            e = pltpu.roll(e, CHUNK, 1)
        return jnp.where(low & (c * CHUNK + lane < live_rows), e, 0.0)

    def panels(c, s, common):
        walker = c * CHUNK + jnp.where(low, lane, lane - CHUNK)
        d = jnp.where(walker < live_rows, s - common, 0.0)
        erow = energies(c)
        return d, erow, (d + pltpu.roll(d * erow, CHUNK, 1)).astype(BF16)

    def own_side(c, d, erow):
        own = jnp.where(low, d, 0.0)
        hi, lo = two_terms(own)
        lhs[c] = jnp.concatenate(
            [
                hi, lo, first_low,
                pltpu.roll(hi, CHUNK, 1), pltpu.roll(lo, CHUNK, 1), first_high,
            ],
            axis=0,
        ).astype(BF16)
        return exact_dot(jnp.where(row8 == 3, erow, mark(2, 0, CHUNK)), own, NT)

    def send_all(src, dst, send_sem, recv_sem):
        for peer in blk_peers:
            pltpu.make_async_remote_copy(
                src_ref=src, dst_ref=dst, send_sem=send_sem, recv_sem=recv_sem,
                device_id=(w, peer), device_id_type=MESH,
            ).start()

    s0 = project(0)
    pmean = jnp.sum(jnp.where(low, s0, 0.0), axis=1, keepdims=True) * (1.0 / CHUNK)
    qmean = jnp.sum(jnp.where(low, 0.0, s0), axis=1, keepdims=True) * (1.0 / CHUNK)
    phi, plo = two_terms(pmean)
    qhi, qlo = two_terms(qmean)
    common = jnp.where(low, phi + plo, qhi + qlo)
    shift = jnp.where(
        lane == 0, phi, jnp.where(lane == 1, plo, jnp.where(lane == 2, qhi, jnp.where(lane == 3, qlo, 0.0)))
    )
    s1 = project(1)
    en_copy.wait()
    d0, e0, g0 = panels(0, s0, common)
    d1, e1, g1 = panels(1, s1, common)
    panel[b, 0] = g0
    panel[b, 1] = g1
    panel[b, 2] = shift.astype(BF16)
    pl.semaphore_wait(barrier, nw - 1 + nb - 1)
    send_all(panel.at[b], panel.at[b], asend, arecv)

    s2 = project(2)
    d2, e2, g2 = panels(2, s2, common)
    tail[b] = g2
    send_all(tail.at[b], tail.at[b], bsend, brecv)

    lhs[chunks] = jnp.concatenate(
        [blank, blank, mark(1, 0, 2), blank, blank, mark(1, 2, 4)], axis=0
    ).astype(BF16)
    rv = own_side(0, d0, e0) + own_side(1, d1, e1) + own_side(2, d2, e2)
    rv = rv + exact_dot(mark(4, 0, 2), shift, NT)
    rv = jnp.concatenate([rv, jnp.zeros((8, LANES - dirs), F32)], axis=1)
    esum = jnp.sum(e0 + e1 + e2, axis=1, keepdims=True)
    small = rv + jnp.where(
        row8 == 5, esum, jnp.where(row8 == 6, live_rows.astype(F32), 0.0)
    )

    def gram_of(c, block):
        return lax.dot_general(
            lhs[c], block.reshape(nb * dirs, LANES), NT, preferred_element_type=F32
        )

    others = pl.ds(0, nb - 1)
    pltpu.make_async_copy(panel.at[others], panel.at[others], arecv).wait()
    gram = gram_of(0, panel[:, 0]) + gram_of(1, panel[:, 1]) + gram_of(chunks, panel[:, 2])
    pltpu.make_async_copy(tail.at[others], tail.at[others], brecv).wait()
    gram = gram + gram_of(2, tail[...])

    for t in range(nb * dirs // LANES):
        tile = gram[:, t * LANES : (t + 1) * LANES]
        sums = []
        for part in (tile[:tall], tile[tall:]):
            sums.append(
                jnp.concatenate([part[:dirs] + part[dirs : 2 * dirs], part[2 * dirs :]], axis=0)
            )
        cpart, hpart = sums
        for i, both in enumerate(
            (
                jnp.where(low, cpart, pltpu.roll(hpart, CHUNK, 1)),
                jnp.where(low, pltpu.roll(cpart, CHUNK, 1), hpart),
            )
        ):
            hi, lo = two_terms(both[dirs:] + small)
            msg[2 * t + i] = jnp.concatenate([both[:dirs], hi, lo], axis=0).astype(BF16)
    for peer in walk_peers:
        pltpu.make_async_remote_copy(
            src_ref=msg.at[peer], dst_ref=got.at[w], send_sem=msend, recv_sem=mrecv,
            device_id=(peer, b), device_id_type=MESH,
        ).start()
    got[w] = msg[w]

    pltpu.make_async_copy(panel.at[others], panel.at[others], asend).wait()
    pltpu.make_async_copy(tail.at[others], tail.at[others], bsend).wait()
    groups = pl.ds(0, nw - 1)
    pltpu.make_async_copy(got.at[groups], got.at[groups], mrecv).wait()

    total = jnp.zeros((dirs, LANES), F32)
    for i in range(nw):
        one = got[i].astype(F32)
        total = total + one[:dirs]
        vecs[i] = one[dirs : dirs + 8] + one[dirs + 8 :]
    jsum, jshift = vecs[:, 0], vecs[:, 1]
    isum, usum, ishift = vecs[:, 2, :dirs], vecs[:, 3, :dirs], vecs[:, 4, :dirs]
    esum, live = vecs[:, 5], vecs[:, 6]
    inv = 1.0 / jnp.sum(live, axis=0, keepdims=True)
    jref = jnp.sum(jnp.where(low, jsum, 0.0) + live * jshift, axis=0, keepdims=True) * inv
    iref = (
        jnp.sum(isum + live[:, :dirs] * ishift, axis=0, keepdims=True) * inv[:, :dirs]
    )
    jdiff = jshift - jref
    pdiff = jnp.where(low, 0.0, pltpu.roll(jdiff, CHUNK, 1))
    left = jnp.concatenate([usum, isum, ishift - iref], axis=0)
    right = jnp.concatenate([pdiff, jdiff, jsum + live * jdiff + esum * pdiff], axis=0)
    o_ref[...] = (total + exact_dot(left, right, TN)) * inv
    pltpu.make_async_copy(got.at[groups], got.at[groups], msend).wait()


def solution(mesh):
    nw, nb = mesh.shape["walk"], mesh.shape["blk"]

    def per_device(derivs, energy_grads, local_energy, directions, widths, live_rows):
        rows, cols = derivs.shape
        dirs = directions.shape[0]
        chunks = rows // CHUNK
        hbm_spec = pl.BlockSpec(memory_space=pltpu.HBM)
        smem_spec = pl.BlockSpec(memory_space=pltpu.SMEM)
        dma = pltpu.SemaphoreType.DMA
        out = pl.pallas_call(
            functools.partial(pencil_kernel, nw, nb),
            out_shape=jax.ShapeDtypeStruct((dirs, LANES), F32),
            in_specs=[hbm_spec] * 4 + [smem_spec] * 2,
            out_specs=pl.BlockSpec(memory_space=pltpu.VMEM),
            scratch_shapes=[
                pltpu.VMEM((rows, cols), BF16),
                pltpu.VMEM((rows, cols), BF16),
                pltpu.VMEM((dirs, cols), BF16),
                pltpu.VMEM((1, rows), F32),
                pltpu.VMEM((nb, EARLY + 1, dirs, LANES), BF16),
                pltpu.VMEM((nb, dirs, LANES), BF16),
                pltpu.VMEM((chunks + 1, 4 * dirs + 16, LANES), BF16),
                pltpu.VMEM((nw, dirs + 16, LANES), BF16),
                pltpu.VMEM((nw, dirs + 16, LANES), BF16),
                pltpu.VMEM((nw, 8, LANES), F32),
                dma((chunks * SPLIT,)),
                dma((chunks * SPLIT,)),
                dma((SPLIT,)),
            ]
            + [dma(())] * 7,
            compiler_params=pltpu.CompilerParams(
                collective_id=0, has_side_effects=True, vmem_limit_bytes=53 << 20
            ),
            name="pencil",
        )(
            derivs, energy_grads, directions, local_energy.reshape(1, rows), widths, live_rows
        )
        return out[:, CHUNK:], out[:, :CHUNK]

    return jax.shard_map(
        per_device,
        mesh=mesh,
        in_specs=(
            P("walk", "blk"), P("walk", "blk"), P("walk"), P("blk", None), P("blk"), P("walk"),
        ),
        out_specs=(P("blk", "walk"), P("blk", "walk")),
        check_vma=False,
    )
```

```python
import functools

import jax
import jax.numpy as jnp
from jax import lax
from jax.experimental import pallas as pl
from jax.experimental.pallas import tpu as pltpu
from jax.sharding import PartitionSpec as P

MESH = pl.DeviceIdType.MESH
F32 = jnp.float32
BF16 = jnp.bfloat16
CHUNK = 64
LANES = 128
SPLIT = 2
AHEAD = 3
NT = (((1,), (1,)), ((), ()))
TN = (((0,), (0,)), ((), ()))


def exact_dot(a, b, dims):
    return lax.dot_general(
        a, b, dims, precision=lax.Precision.HIGHEST, preferred_element_type=F32
    )


def two_terms(x):
    hi = x.astype(BF16).astype(F32)
    return hi, (x - hi).astype(BF16).astype(F32)


def ring_peers(me, count, inner):
    outer = count // inner
    hops = lambda n, size: min(n, size - n)
    steps = [(i, j) for i in range(outer) for j in range(inner) if (i, j) != (0, 0)]
    steps.sort(key=lambda s: -(hops(s[0], outer) + hops(s[1], inner)))
    major, minor = me // inner, lax.rem(me, inner)
    return [
        lax.rem(major + i, outer) * inner + lax.rem(minor + j, inner) for i, j in steps
    ]


def pencil_kernel(
    nw, nb, d_hbm, e_hbm, v_hbm, en_hbm, wid_ref, live_ref, o_ref,
    dv, ev, vv, en_ref, panel, middle, tail, lhs, base, msg, got, vecs,
    dsem, esem, vsem, brecv, ensem, asend, arecv, csend, crecv, bsend, msend, mrecv,
):
    w = lax.axis_index("walk")
    b = lax.axis_index("blk")
    rows, cols = d_hbm.shape
    dirs = v_hbm.shape[0]
    width = cols // SPLIT
    chunks = rows // CHUNK
    pieces = [(c, k) for c in range(chunks) for k in range(SPLIT)]

    quarter = width // 2

    def dir_copy(k):
        part = (slice(None), pl.ds(k * quarter, quarter))
        return pltpu.make_async_copy(v_hbm.at[part], vv.at[part], vsem.at[k])

    def piece_copies(i):
        c, k = pieces[i]
        part = (pl.ds(c * CHUNK, CHUNK), pl.ds(k * width, width))
        return (
            pltpu.make_async_copy(d_hbm.at[part], dv.at[part], dsem.at[i]),
            pltpu.make_async_copy(e_hbm.at[part], ev.at[part], esem.at[i]),
        )

    def start_piece(i):
        if i < SPLIT:
            dir_copy(2 * i).start()
            dir_copy(2 * i + 1).start()
        for copy in piece_copies(i):
            copy.start()

    en_copy = pltpu.make_async_copy(en_hbm, en_ref, ensem)
    for i in range(AHEAD):
        start_piece(i)
    en_copy.start()

    walk_peers = ring_peers(w, nw, 2)
    blk_peers = ring_peers(b, nb, 4)
    barrier = pltpu.get_barrier_semaphore()
    for peer in blk_peers:
        pl.semaphore_signal(barrier, inc=1, device_id=(w, peer), device_id_type=MESH)
    for peer in walk_peers:
        pl.semaphore_signal(barrier, inc=1, device_id=(peer, b), device_id_type=MESH)

    lane = lax.broadcasted_iota(jnp.int32, (1, LANES), 1)
    low = lane < CHUNK
    used = wid_ref[0]
    live_rows = live_ref[0]

    def project(c):
        total = None
        for k in range(SPLIT):
            i = c * SPLIT + k
            span = pl.ds(k * width, width)
            if c == 0:
                for q in (2 * k, 2 * k + 1):
                    dir_copy(q).wait()
                    part = pl.ds(q * quarter, quarter)
                    column = lax.broadcasted_iota(jnp.int32, (1, quarter), 1) + q * quarter
                    vv[:, part] = vv[:, part] * jnp.where(column < used, 1.0, 0.0).astype(BF16)
            for copy in piece_copies(i):
                copy.wait()
            if i + AHEAD < len(pieces):
                start_piece(i + AHEAD)
            rs = pl.ds(c * CHUNK, CHUNK)
            weights = vv[:, span]
            part = jnp.concatenate(
                [
                    lax.dot_general(weights, dv[rs, span], NT, preferred_element_type=F32),
                    lax.dot_general(weights, ev[rs, span], NT, preferred_element_type=F32),
                ],
                axis=1,
            )
            total = part if total is None else total + part
        return total

    row8 = lax.broadcasted_iota(jnp.int32, (8, LANES), 0)
    lane8 = lax.broadcasted_iota(jnp.int32, (8, LANES), 1)

    def mark(row, lo, hi):
        return jnp.where((row8 == row) & (lane8 >= lo) & (lane8 < hi), 1.0, 0.0)

    first_low = mark(0, 0, CHUNK)
    first_high = mark(0, CHUNK, LANES)
    blank = jnp.zeros((dirs, LANES), F32)
    tall = 2 * dirs + 8

    def energies(c):
        lo = (c * CHUNK) // LANES * LANES
        if lo + LANES > rows:
            e = jnp.concatenate(
                [en_ref[:, lo:rows], jnp.zeros((1, LANES - (rows - lo)), F32)], axis=1
            )
        else:
            e = en_ref[:, lo : lo + LANES]
        if c % 2:
            e = pltpu.roll(e, CHUNK, 1)
        return jnp.where(low & (c * CHUNK + lane < live_rows), e, 0.0)

    def panels(c, s, common):
        walker = c * CHUNK + jnp.where(low, lane, lane - CHUNK)
        d = jnp.where(walker < live_rows, s - common, 0.0)
        erow = energies(c)
        return d, erow, (d + pltpu.roll(d * erow, CHUNK, 1)).astype(BF16)

    def own_side(c, d, erow):
        own = jnp.where(low, d, 0.0)
        hi, lo = two_terms(own)
        lhs[c] = jnp.concatenate(
            [
                hi, lo, first_low,
                pltpu.roll(hi, CHUNK, 1), pltpu.roll(lo, CHUNK, 1), first_high,
            ],
            axis=0,
        ).astype(BF16)
        return exact_dot(jnp.where(row8 == 3, erow, mark(2, 0, CHUNK)), own, NT)

    def send_all(buf, send_sem, recv_sem):
        for peer in blk_peers:
            pltpu.make_async_remote_copy(
                src_ref=buf.at[b], dst_ref=buf.at[b], send_sem=send_sem, recv_sem=recv_sem,
                device_id=(w, peer), device_id_type=MESH,
            ).start()

    s0 = project(0)
    pmean = jnp.sum(jnp.where(low, s0, 0.0), axis=1, keepdims=True) * (1.0 / CHUNK)
    qmean = jnp.sum(jnp.where(low, 0.0, s0), axis=1, keepdims=True) * (1.0 / CHUNK)
    phi, plo = two_terms(pmean)
    qhi, qlo = two_terms(qmean)
    common = jnp.where(low, phi + plo, qhi + qlo)
    shift = jnp.where(
        lane == 0, phi, jnp.where(lane == 1, plo, jnp.where(lane == 2, qhi, jnp.where(lane == 3, qlo, 0.0)))
    )
    en_copy.wait()
    d0, e0, g0 = panels(0, s0, common)
    panel[b, 0] = g0
    panel[b, 1] = shift.astype(BF16)
    pl.semaphore_wait(barrier, nw - 1 + nb - 1)
    send_all(panel, asend, arecv)

    d1, e1, g1 = panels(1, project(1), common)
    middle[b] = g1
    send_all(middle, csend, crecv)

    d2, e2, g2 = panels(2, project(2), common)
    tail[b] = g2
    send_all(tail, bsend, brecv.at[b])

    lhs[chunks] = jnp.concatenate(
        [blank, blank, mark(1, 0, 2), blank, blank, mark(1, 2, 4)], axis=0
    ).astype(BF16)
    rv = own_side(0, d0, e0) + own_side(1, d1, e1) + own_side(2, d2, e2)
    rv = rv + exact_dot(mark(4, 0, 2), shift, NT)
    rv = jnp.concatenate([rv, jnp.zeros((8, LANES - dirs), F32)], axis=1)
    esum = jnp.sum(e0 + e1 + e2, axis=1, keepdims=True)
    small = rv + jnp.where(
        row8 == 5, esum, jnp.where(row8 == 6, live_rows.astype(F32), 0.0)
    )

    def gram_of(c, block, count):
        return lax.dot_general(
            lhs[c], block.reshape(count * dirs, LANES), NT, preferred_element_type=F32
        )

    def halves_of(tile):
        return [
            jnp.concatenate([part[:dirs] + part[dirs : 2 * dirs], part[2 * dirs :]], axis=0)
            for part in (tile[:tall], tile[tall:])
        ]

    others = pl.ds(0, nb - 1)
    pltpu.make_async_copy(panel.at[others], panel.at[others], arecv).wait()
    gram = gram_of(0, panel[:, 0], nb) + gram_of(chunks, panel[:, 1], nb)
    pltpu.make_async_copy(middle.at[others], middle.at[others], crecv).wait()
    gram = gram + gram_of(1, middle[...], nb)
    extra = jnp.concatenate([blank, small], axis=0)
    for t in range(nw // 2):
        cpart, hpart = halves_of(gram[:, t * LANES : (t + 1) * LANES])
        base[2 * t] = jnp.where(low, cpart, pltpu.roll(hpart, CHUNK, 1)) + extra
        base[2 * t + 1] = jnp.where(low, pltpu.roll(cpart, CHUNK, 1), hpart) + extra

    outer = nb // 4
    order = [(i, j) for i in range(outer) for j in range(2)]
    order.sort(key=lambda s: min(s[0], outer - s[0]) + s[1])
    for i, j in order:
        to = lax.rem(b // 4 + i, outer) * 2 + lax.rem(lax.rem(b, 4) // 2 + j, 2)
        for src in (2 * to, 2 * to + 1):

            @pl.when(src != b)
            def _():
                pltpu.make_async_copy(tail.at[src], tail.at[src], brecv.at[src]).wait()

        both = base[to] + jnp.concatenate(
            halves_of(gram_of(2, tail[pl.ds(2 * to, 2)], 2)), axis=1
        )
        hi, lo = two_terms(both[dirs:])
        msg[to] = jnp.concatenate([both[:dirs], hi, lo], axis=0).astype(BF16)

        @pl.when(to != w)
        def _():
            pltpu.make_async_remote_copy(
                src_ref=msg.at[to], dst_ref=got.at[w], send_sem=msend, recv_sem=mrecv,
                device_id=(to, b), device_id_type=MESH,
            ).start()

    got[w] = msg[w]

    pltpu.make_async_copy(panel.at[others], panel.at[others], asend).wait()
    pltpu.make_async_copy(middle.at[others], middle.at[others], csend).wait()
    pltpu.make_async_copy(tail.at[others], tail.at[others], bsend).wait()
    groups = pl.ds(0, nw - 1)
    pltpu.make_async_copy(got.at[groups], got.at[groups], mrecv).wait()

    total = jnp.zeros((dirs, LANES), F32)
    for i in range(nw):
        one = got[i].astype(F32)
        total = total + one[:dirs]
        vecs[i] = one[dirs : dirs + 8] + one[dirs + 8 :]
    jsum, jshift = vecs[:, 0], vecs[:, 1]
    isum, usum, ishift = vecs[:, 2, :dirs], vecs[:, 3, :dirs], vecs[:, 4, :dirs]
    esum, live = vecs[:, 5], vecs[:, 6]
    inv = 1.0 / jnp.sum(live, axis=0, keepdims=True)
    jref = jnp.sum(jnp.where(low, jsum, 0.0) + live * jshift, axis=0, keepdims=True) * inv
    iref = (
        jnp.sum(isum + live[:, :dirs] * ishift, axis=0, keepdims=True) * inv[:, :dirs]
    )
    jdiff = jshift - jref
    pdiff = jnp.where(low, 0.0, pltpu.roll(jdiff, CHUNK, 1))
    left = jnp.concatenate([usum, isum, ishift - iref], axis=0)
    right = jnp.concatenate([pdiff, jdiff, jsum + live * jdiff + esum * pdiff], axis=0)
    o_ref[...] = (total + exact_dot(left, right, TN)) * inv
    pltpu.make_async_copy(got.at[groups], got.at[groups], msend).wait()


def solution(mesh):
    nw, nb = mesh.shape["walk"], mesh.shape["blk"]

    def per_device(derivs, energy_grads, local_energy, directions, widths, live_rows):
        rows, cols = derivs.shape
        dirs = directions.shape[0]
        chunks = rows // CHUNK
        hbm_spec = pl.BlockSpec(memory_space=pltpu.HBM)
        smem_spec = pl.BlockSpec(memory_space=pltpu.SMEM)
        dma = pltpu.SemaphoreType.DMA
        out = pl.pallas_call(
            functools.partial(pencil_kernel, nw, nb),
            out_shape=jax.ShapeDtypeStruct((dirs, LANES), F32),
            in_specs=[hbm_spec] * 4 + [smem_spec] * 2,
            out_specs=pl.BlockSpec(memory_space=pltpu.VMEM),
            scratch_shapes=[
                pltpu.VMEM((rows, cols), BF16),
                pltpu.VMEM((rows, cols), BF16),
                pltpu.VMEM((dirs, cols), BF16),
                pltpu.VMEM((1, rows), F32),
                pltpu.VMEM((nb, 2, dirs, LANES), BF16),
                pltpu.VMEM((nb, dirs, LANES), BF16),
                pltpu.VMEM((nb, dirs, LANES), BF16),
                pltpu.VMEM((chunks + 1, 4 * dirs + 16, LANES), BF16),
                pltpu.VMEM((nw, dirs + 8, LANES), F32),
                pltpu.VMEM((nw, dirs + 16, LANES), BF16),
                pltpu.VMEM((nw, dirs + 16, LANES), BF16),
                pltpu.VMEM((nw, 8, LANES), F32),
                dma((chunks * SPLIT,)),
                dma((chunks * SPLIT,)),
                dma((2 * SPLIT,)),
                dma((nb,)),
            ]
            + [dma(())] * 8,
            compiler_params=pltpu.CompilerParams(
                collective_id=0, has_side_effects=True, vmem_limit_bytes=53 << 20
            ),
            name="pencil",
        )(
            derivs, energy_grads, directions,
            pltpu.with_memory_space_constraint(local_energy.reshape(1, rows), pltpu.HBM),
            widths, live_rows,
        )
        return out[:, CHUNK:], out[:, :CHUNK]

    return jax.shard_map(
        per_device,
        mesh=mesh,
        in_specs=(
            P("walk", "blk"), P("walk", "blk"), P("walk"), P("blk", None), P("blk"), P("walk"),
        ),
        out_specs=(P("blk", "walk"), P("blk", "walk")),
        check_vma=False,
    )
```

```python
import functools

import jax
import jax.numpy as jnp
from jax import lax
from jax.experimental import pallas as pl
from jax.experimental.pallas import tpu as pltpu
from jax.sharding import PartitionSpec as P

MESH = pl.DeviceIdType.MESH
F32 = jnp.float32
BF16 = jnp.bfloat16
CHUNK = 64
LANES = 128
SPLIT = 2
AHEAD = 3
NT = (((1,), (1,)), ((), ()))
TN = (((0,), (0,)), ((), ()))


def exact_dot(a, b, dims):
    return lax.dot_general(
        a, b, dims, precision=lax.Precision.HIGHEST, preferred_element_type=F32
    )


def two_terms(x):
    hi = x.astype(BF16).astype(F32)
    return hi, (x - hi).astype(BF16).astype(F32)


def ring_peers(me, count, inner):
    outer = count // inner
    hops = lambda n, size: min(n, size - n)
    steps = [(i, j) for i in range(outer) for j in range(inner) if (i, j) != (0, 0)]
    steps.sort(key=lambda s: -(hops(s[0], outer) + hops(s[1], inner)))
    major, minor = me // inner, lax.rem(me, inner)
    return [
        lax.rem(major + i, outer) * inner + lax.rem(minor + j, inner) for i, j in steps
    ]


def pencil_kernel(
    nw, nb, d_hbm, e_hbm, v_hbm, en_hbm, wid_ref, live_ref, o_ref,
    dv, ev, vv, en_ref, panel, tail, lhs, msg, got, vecs,
    dsem, esem, vsem, arecv, brecv, ensem, asend, csend, bsend, msend, mrecv,
):
    w = lax.axis_index("walk")
    b = lax.axis_index("blk")
    rows, cols = d_hbm.shape
    dirs = v_hbm.shape[0]
    width = cols // SPLIT
    chunks = rows // CHUNK
    pieces = [(c, k) for c in range(chunks) for k in range(SPLIT)]

    quarter = width // 2

    def dir_copy(k):
        part = (slice(None), pl.ds(k * quarter, quarter))
        return pltpu.make_async_copy(v_hbm.at[part], vv.at[part], vsem.at[k])

    def piece_copies(i):
        c, k = pieces[i]
        part = (pl.ds(c * CHUNK, CHUNK), pl.ds(k * width, width))
        return (
            pltpu.make_async_copy(d_hbm.at[part], dv.at[part], dsem.at[i]),
            pltpu.make_async_copy(e_hbm.at[part], ev.at[part], esem.at[i]),
        )

    def start_piece(i):
        if i < SPLIT:
            dir_copy(2 * i).start()
            dir_copy(2 * i + 1).start()
        for copy in piece_copies(i):
            copy.start()

    en_copy = pltpu.make_async_copy(en_hbm, en_ref, ensem)
    for i in range(AHEAD):
        start_piece(i)
    en_copy.start()

    walk_peers = ring_peers(w, nw, 2)
    blk_peers = ring_peers(b, nb, 4)
    barrier = pltpu.get_barrier_semaphore()
    for peer in blk_peers:
        pl.semaphore_signal(barrier, inc=1, device_id=(w, peer), device_id_type=MESH)
    for peer in walk_peers:
        pl.semaphore_signal(barrier, inc=1, device_id=(peer, b), device_id_type=MESH)

    lane = lax.broadcasted_iota(jnp.int32, (1, LANES), 1)
    low = lane < CHUNK
    used = wid_ref[0]
    live_rows = live_ref[0]

    def project(c):
        total = None
        for k in range(SPLIT):
            i = c * SPLIT + k
            span = pl.ds(k * width, width)
            if c == 0:
                for q in (2 * k, 2 * k + 1):
                    dir_copy(q).wait()
                    part = pl.ds(q * quarter, quarter)
                    column = lax.broadcasted_iota(jnp.int32, (1, quarter), 1) + q * quarter
                    vv[:, part] = vv[:, part] * jnp.where(column < used, 1.0, 0.0).astype(BF16)
            for copy in piece_copies(i):
                copy.wait()
            if i + AHEAD < len(pieces):
                start_piece(i + AHEAD)
            rs = pl.ds(c * CHUNK, CHUNK)
            weights = vv[:, span]
            part = jnp.concatenate(
                [
                    lax.dot_general(weights, dv[rs, span], NT, preferred_element_type=F32),
                    lax.dot_general(weights, ev[rs, span], NT, preferred_element_type=F32),
                ],
                axis=1,
            )
            total = part if total is None else total + part
        return total

    row8 = lax.broadcasted_iota(jnp.int32, (8, LANES), 0)
    lane8 = lax.broadcasted_iota(jnp.int32, (8, LANES), 1)

    def mark(row, lo, hi):
        return jnp.where((row8 == row) & (lane8 >= lo) & (lane8 < hi), 1.0, 0.0)

    first_low = mark(0, 0, CHUNK)
    first_high = mark(0, CHUNK, LANES)
    blank = jnp.zeros((dirs, LANES), F32)
    tall = 2 * dirs + 8

    def energies(c):
        lo = (c * CHUNK) // LANES * LANES
        if lo + LANES > rows:
            e = jnp.concatenate(
                [en_ref[:, lo:rows], jnp.zeros((1, LANES - (rows - lo)), F32)], axis=1
            )
        else:
            e = en_ref[:, lo : lo + LANES]
        if c % 2:
            e = pltpu.roll(e, CHUNK, 1)
        return jnp.where(low & (c * CHUNK + lane < live_rows), e, 0.0)

    def panels(c, s, common):
        walker = c * CHUNK + jnp.where(low, lane, lane - CHUNK)
        d = jnp.where(walker < live_rows, s - common, 0.0)
        erow = energies(c)
        return d, erow, (d + pltpu.roll(d * erow, CHUNK, 1)).astype(BF16)

    def own_side(c, d, erow):
        own = jnp.where(low, d, 0.0)
        hi, lo = two_terms(own)
        lhs[c] = jnp.concatenate(
            [
                hi, lo, first_low,
                pltpu.roll(hi, CHUNK, 1), pltpu.roll(lo, CHUNK, 1), first_high,
            ],
            axis=0,
        ).astype(BF16)
        return exact_dot(jnp.where(row8 == 3, erow, mark(2, 0, CHUNK)), own, NT)

    def send_all(buf, send_sem, recv_sem):
        for peer in blk_peers:
            pltpu.make_async_remote_copy(
                src_ref=buf, dst_ref=buf, send_sem=send_sem, recv_sem=recv_sem.at[b // 4],
                device_id=(w, peer), device_id_type=MESH,
            ).start()

    s0 = project(0)
    pmean = jnp.sum(jnp.where(low, s0, 0.0), axis=1, keepdims=True) * (1.0 / CHUNK)
    qmean = jnp.sum(jnp.where(low, 0.0, s0), axis=1, keepdims=True) * (1.0 / CHUNK)
    phi, plo = two_terms(pmean)
    qhi, qlo = two_terms(qmean)
    common = jnp.where(low, phi + plo, qhi + qlo)
    shift = jnp.where(
        lane == 0, phi, jnp.where(lane == 1, plo, jnp.where(lane == 2, qhi, jnp.where(lane == 3, qlo, 0.0)))
    )
    en_copy.wait()
    d0, e0, g0 = panels(0, s0, common)
    panel[b, dirs : 2 * dirs] = g0
    panel[b, 2 * dirs :] = (
        shift[: dirs // 2] + pltpu.roll(shift[dirs // 2 :], CHUNK, 1)
    ).astype(BF16)
    pl.semaphore_wait(barrier, nw - 1 + nb - 1)
    send_all(panel.at[b, dirs:], asend, arecv)

    d1, e1, g1 = panels(1, project(1), common)
    panel[b, :dirs] = g1
    send_all(panel.at[b, :dirs], csend, arecv)

    d2, e2, g2 = panels(2, project(2), common)
    tail[b] = g2
    send_all(tail.at[b], bsend, brecv)

    lhs[chunks] = jnp.concatenate(
        [blank, blank, mark(1, 0, 2), blank, blank, mark(1, 2, 4)], axis=0
    ).astype(BF16)
    rv = own_side(0, d0, e0) + own_side(1, d1, e1) + own_side(2, d2, e2)
    rv = rv + exact_dot(mark(4, 0, 2), shift, NT)
    rv = jnp.concatenate([rv, jnp.zeros((8, LANES - dirs), F32)], axis=1)
    esum = jnp.sum(e0 + e1 + e2, axis=1, keepdims=True)
    small = rv + jnp.where(
        row8 == 5, esum, jnp.where(row8 == 6, live_rows.astype(F32), 0.0)
    )

    def gram_of(c, block):
        return lax.dot_general(
            lhs[c], block.reshape(4 * dirs, LANES), NT, preferred_element_type=F32
        )

    def halves_of(tile):
        return [
            jnp.concatenate([part[:dirs] + part[dirs : 2 * dirs], part[2 * dirs :]], axis=0)
            for part in (tile[:tall], tile[tall:])
        ]

    def arrival(buf, sem, t):
        def take(count):
            part = buf.at[pl.ds(4 * t, count)]
            pltpu.make_async_copy(part, part, sem.at[t]).wait()

        pl.when(t == b // 4)(lambda: take(3))
        pl.when(t != b // 4)(lambda: take(4))

    for t in range(nb // 4):
        quad = slice(4 * t, 4 * t + 4)
        arrival(panel, arecv, t)
        packed = panel[quad, 2 * dirs :].astype(F32)
        packed = jnp.concatenate([packed, pltpu.roll(packed, CHUNK, 2)], axis=1).astype(BF16)
        early = (
            gram_of(0, panel[quad, dirs : 2 * dirs])
            + gram_of(chunks, packed)
            + gram_of(1, panel[quad, :dirs])
        )
        arrival(tail, brecv, t)
        cpart, hpart = halves_of(early + gram_of(2, tail[quad]))
        for i, both in enumerate(
            (
                jnp.where(low, cpart, pltpu.roll(hpart, CHUNK, 1)),
                jnp.where(low, pltpu.roll(cpart, CHUNK, 1), hpart),
            )
        ):
            to = 2 * t + i
            hi, lo = two_terms(both[dirs:] + small)
            msg[to] = jnp.concatenate([both[:dirs], hi, lo], axis=0).astype(BF16)

            @pl.when(to != w)
            def _():
                pltpu.make_async_remote_copy(
                    src_ref=msg.at[to], dst_ref=got.at[w], send_sem=msend, recv_sem=mrecv,
                    device_id=(to, b), device_id_type=MESH,
                ).start()

    got[w] = msg[w]

    others = pl.ds(0, nb - 1)
    for part, sem in ((panel.at[others, dirs:], asend), (panel.at[others, :dirs], csend)):
        pltpu.make_async_copy(part, part, sem).wait()
    pltpu.make_async_copy(tail.at[others], tail.at[others], bsend).wait()
    groups = pl.ds(0, nw - 1)
    pltpu.make_async_copy(got.at[groups], got.at[groups], mrecv).wait()

    total = jnp.zeros((dirs, LANES), F32)
    for i in range(nw):
        one = got[i].astype(F32)
        total = total + one[:dirs]
        vecs[i] = one[dirs : dirs + 8] + one[dirs + 8 :]
    jsum, jshift = vecs[:, 0], vecs[:, 1]
    isum, usum, ishift = vecs[:, 2, :dirs], vecs[:, 3, :dirs], vecs[:, 4, :dirs]
    esum, live = vecs[:, 5], vecs[:, 6]
    inv = 1.0 / jnp.sum(live, axis=0, keepdims=True)
    jref = jnp.sum(jnp.where(low, jsum, 0.0) + live * jshift, axis=0, keepdims=True) * inv
    iref = (
        jnp.sum(isum + live[:, :dirs] * ishift, axis=0, keepdims=True) * inv[:, :dirs]
    )
    jdiff = jshift - jref
    pdiff = jnp.where(low, 0.0, pltpu.roll(jdiff, CHUNK, 1))
    left = jnp.concatenate([usum, isum, ishift - iref], axis=0)
    right = jnp.concatenate([pdiff, jdiff, jsum + live * jdiff + esum * pdiff], axis=0)
    o_ref[...] = (total + exact_dot(left, right, TN)) * inv
    pltpu.make_async_copy(got.at[groups], got.at[groups], msend).wait()


def solution(mesh):
    nw, nb = mesh.shape["walk"], mesh.shape["blk"]

    def per_device(derivs, energy_grads, local_energy, directions, widths, live_rows):
        rows, cols = derivs.shape
        dirs = directions.shape[0]
        chunks = rows // CHUNK
        hbm_spec = pl.BlockSpec(memory_space=pltpu.HBM)
        smem_spec = pl.BlockSpec(memory_space=pltpu.SMEM)
        dma = pltpu.SemaphoreType.DMA
        out = pl.pallas_call(
            functools.partial(pencil_kernel, nw, nb),
            out_shape=jax.ShapeDtypeStruct((dirs, LANES), F32),
            in_specs=[hbm_spec] * 4 + [smem_spec] * 2,
            out_specs=pl.BlockSpec(memory_space=pltpu.VMEM),
            scratch_shapes=[
                pltpu.VMEM((rows, cols), BF16),
                pltpu.VMEM((rows, cols), BF16),
                pltpu.VMEM((dirs, cols), BF16),
                pltpu.VMEM((1, rows), F32),
                pltpu.VMEM((nb, 2 * dirs + dirs // 2, LANES), BF16),
                pltpu.VMEM((nb, dirs, LANES), BF16),
                pltpu.VMEM((chunks + 1, 4 * dirs + 16, LANES), BF16),
                pltpu.VMEM((nw, dirs + 16, LANES), BF16),
                pltpu.VMEM((nw, dirs + 16, LANES), BF16),
                pltpu.VMEM((nw, 8, LANES), F32),
                dma((chunks * SPLIT,)),
                dma((chunks * SPLIT,)),
                dma((2 * SPLIT,)),
                dma((nb // 4,)),
                dma((nb // 4,)),
            ]
            + [dma(())] * 6,
            compiler_params=pltpu.CompilerParams(
                collective_id=0, has_side_effects=True, vmem_limit_bytes=53 << 20
            ),
            name="pencil",
        )(
            derivs, energy_grads, directions,
            pltpu.with_memory_space_constraint(local_energy.reshape(1, rows), pltpu.HBM),
            widths, live_rows,
        )
        return out[:, CHUNK:], out[:, :CHUNK]

    return jax.shard_map(
        per_device,
        mesh=mesh,
        in_specs=(
            P("walk", "blk"), P("walk", "blk"), P("walk"), P("blk", None), P("blk"), P("walk"),
        ),
        out_specs=(P("blk", "walk"), P("blk", "walk")),
        check_vma=False,
    )
```

```python
import functools

import jax
import jax.numpy as jnp
from jax import lax
from jax.experimental import pallas as pl
from jax.experimental.pallas import tpu as pltpu
from jax.sharding import PartitionSpec as P

MESH = pl.DeviceIdType.MESH
F32 = jnp.float32
BF16 = jnp.bfloat16
CHUNK = 64
LANES = 128
SPLIT = 2
AHEAD = 3
NT = (((1,), (1,)), ((), ()))
TN = (((0,), (0,)), ((), ()))


def exact_dot(a, b, dims):
    return lax.dot_general(
        a, b, dims, precision=lax.Precision.HIGHEST, preferred_element_type=F32
    )


def two_terms(x):
    hi = x.astype(BF16).astype(F32)
    return hi, (x - hi).astype(BF16).astype(F32)


def ring_peers(me, count, inner):
    outer = count // inner
    hops = lambda n, size: min(n, size - n)
    steps = [(i, j) for i in range(outer) for j in range(inner) if (i, j) != (0, 0)]
    steps.sort(key=lambda s: -(hops(s[0], outer) + hops(s[1], inner)))
    major, minor = me // inner, lax.rem(me, inner)
    return [
        lax.rem(major + i, outer) * inner + lax.rem(minor + j, inner) for i, j in steps
    ]


def pencil_kernel(
    nw, nb, d_hbm, e_hbm, v_hbm, en_hbm, wid_ref, live_ref, o_ref,
    dv, ev, vv, en_ref, panel, tail, lhs, msg, got, vecs,
    dsem, esem, vsem, arecv, brecv, ensem, asend, csend, bsend, msend, mrecv,
):
    w = lax.axis_index("walk")
    b = lax.axis_index("blk")
    rows, cols = d_hbm.shape
    dirs = v_hbm.shape[0]
    width = cols // SPLIT
    chunks = rows // CHUNK
    pieces = [(c, k) for c in range(chunks) for k in range(SPLIT)]

    quarter = width // 2

    def dir_copy(k):
        part = (slice(None), pl.ds(k * quarter, quarter))
        return pltpu.make_async_copy(v_hbm.at[part], vv.at[part], vsem.at[k])

    def piece_copies(i):
        c, k = pieces[i]
        part = (pl.ds(c * CHUNK, CHUNK), pl.ds(k * width, width))
        return (
            pltpu.make_async_copy(d_hbm.at[part], dv.at[part], dsem.at[i]),
            pltpu.make_async_copy(e_hbm.at[part], ev.at[part], esem.at[i]),
        )

    def start_piece(i):
        if i < SPLIT:
            dir_copy(2 * i).start()
            dir_copy(2 * i + 1).start()
        for copy in piece_copies(i):
            copy.start()

    en_copy = pltpu.make_async_copy(en_hbm, en_ref, ensem)
    for i in range(AHEAD):
        start_piece(i)
    en_copy.start()

    walk_peers = ring_peers(w, nw, 2)
    blk_peers = ring_peers(b, nb, 4)
    barrier = pltpu.get_barrier_semaphore()
    for peer in blk_peers:
        pl.semaphore_signal(barrier, inc=1, device_id=(w, peer), device_id_type=MESH)
    for peer in walk_peers:
        pl.semaphore_signal(barrier, inc=1, device_id=(peer, b), device_id_type=MESH)

    lane = lax.broadcasted_iota(jnp.int32, (1, LANES), 1)
    low = lane < CHUNK
    used = wid_ref[0]
    live_rows = live_ref[0]

    def project(c):
        total = None
        for k in range(SPLIT):
            i = c * SPLIT + k
            span = pl.ds(k * width, width)
            if c == 0:
                for q in (2 * k, 2 * k + 1):
                    dir_copy(q).wait()
                    part = pl.ds(q * quarter, quarter)
                    column = lax.broadcasted_iota(jnp.int32, (1, quarter), 1) + q * quarter
                    vv[:, part] = vv[:, part] * jnp.where(column < used, 1.0, 0.0).astype(BF16)
            for copy in piece_copies(i):
                copy.wait()
            if i + AHEAD < len(pieces):
                start_piece(i + AHEAD)
            rs = pl.ds(c * CHUNK, CHUNK)
            weights = vv[:, span]
            part = jnp.concatenate(
                [
                    lax.dot_general(weights, dv[rs, span], NT, preferred_element_type=F32),
                    lax.dot_general(weights, ev[rs, span], NT, preferred_element_type=F32),
                ],
                axis=1,
            )
            total = part if total is None else total + part
        return total

    row8 = lax.broadcasted_iota(jnp.int32, (8, LANES), 0)
    lane8 = lax.broadcasted_iota(jnp.int32, (8, LANES), 1)

    def mark(row, lo, hi):
        return jnp.where((row8 == row) & (lane8 >= lo) & (lane8 < hi), 1.0, 0.0)

    first_low = mark(0, 0, CHUNK)
    first_high = mark(0, CHUNK, LANES)
    blank = jnp.zeros((dirs, LANES), F32)
    tall = 2 * dirs + 8

    def energies(c):
        lo = (c * CHUNK) // LANES * LANES
        if lo + LANES > rows:
            e = jnp.concatenate(
                [en_ref[:, lo:rows], jnp.zeros((1, LANES - (rows - lo)), F32)], axis=1
            )
        else:
            e = en_ref[:, lo : lo + LANES]
        if c % 2:
            e = pltpu.roll(e, CHUNK, 1)
        return jnp.where(low & (c * CHUNK + lane < live_rows), e, 0.0)

    def panels(c, s, common, erow):
        walker = c * CHUNK + jnp.where(low, lane, lane - CHUNK)
        d = jnp.where(walker < live_rows, s - common, 0.0)
        return d, (d + pltpu.roll(d * erow, CHUNK, 1)).astype(BF16)

    def own_side(c, d, erow):
        own = jnp.where(low, d, 0.0)
        hi, lo = two_terms(own)
        lhs[c] = jnp.concatenate(
            [
                hi, lo, first_low,
                pltpu.roll(hi, CHUNK, 1), pltpu.roll(lo, CHUNK, 1), first_high,
            ],
            axis=0,
        ).astype(BF16)
        return exact_dot(jnp.where(row8 == 3, erow, mark(2, 0, CHUNK)), own, NT)

    def send_all(buf, send_sem, recv_sem):
        for peer in blk_peers:
            pltpu.make_async_remote_copy(
                src_ref=buf, dst_ref=buf, send_sem=send_sem, recv_sem=recv_sem.at[b // 4],
                device_id=(w, peer), device_id_type=MESH,
            ).start()

    s0 = project(0)
    pmean = jnp.sum(jnp.where(low, s0, 0.0), axis=1, keepdims=True) * (1.0 / CHUNK)
    qmean = jnp.sum(jnp.where(low, 0.0, s0), axis=1, keepdims=True) * (1.0 / CHUNK)
    phi, plo = two_terms(pmean)
    qhi, qlo = two_terms(qmean)
    common = jnp.where(low, phi + plo, qhi + qlo)
    shift = jnp.where(
        lane == 0, phi, jnp.where(lane == 1, plo, jnp.where(lane == 2, qhi, jnp.where(lane == 3, qlo, 0.0)))
    )
    en_copy.wait()
    e0, e1, e2 = energies(0), energies(1), energies(2)
    d0, g0 = panels(0, s0, common, e0)
    panel[b, dirs : 2 * dirs] = g0
    panel[b, 2 * dirs :] = (
        shift[: dirs // 2] + pltpu.roll(shift[dirs // 2 :], CHUNK, 1)
    ).astype(BF16)
    pl.semaphore_wait(barrier, nw - 1 + nb - 1)
    send_all(panel.at[b, dirs:], asend, arecv)

    d1, g1 = panels(1, project(1), common, e1)
    panel[b, :dirs] = g1
    send_all(panel.at[b, :dirs], csend, arecv)

    lhs[chunks] = jnp.concatenate(
        [blank, blank, mark(1, 0, 2), blank, blank, mark(1, 2, 4)], axis=0
    ).astype(BF16)
    rv = own_side(0, d0, e0) + own_side(1, d1, e1) + exact_dot(mark(4, 0, 2), shift, NT)

    d2, g2 = panels(2, project(2), common, e2)
    tail[b] = g2
    send_all(tail.at[b], bsend, brecv)

    rv = rv + own_side(2, d2, e2)
    rv = jnp.concatenate([rv, jnp.zeros((8, LANES - dirs), F32)], axis=1)
    esum = jnp.sum(e0 + e1 + e2, axis=1, keepdims=True)
    small = rv + jnp.where(
        row8 == 5, esum, jnp.where(row8 == 6, live_rows.astype(F32), 0.0)
    )

    def gram_of(c, block):
        return lax.dot_general(
            lhs[c], block.reshape(4 * dirs, LANES), NT, preferred_element_type=F32
        )

    def halves_of(tile):
        return [
            jnp.concatenate([part[:dirs] + part[dirs : 2 * dirs], part[2 * dirs :]], axis=0)
            for part in (tile[:tall], tile[tall:])
        ]

    def arrival(buf, sem, t):
        def take(count):
            part = buf.at[pl.ds(4 * t, count)]
            pltpu.make_async_copy(part, part, sem.at[t]).wait()

        pl.when(t == b // 4)(lambda: take(3))
        pl.when(t != b // 4)(lambda: take(4))

    for t in range(nb // 4):
        quad = slice(4 * t, 4 * t + 4)
        arrival(panel, arecv, t)
        packed = panel[quad, 2 * dirs :].astype(F32)
        packed = jnp.concatenate([packed, pltpu.roll(packed, CHUNK, 2)], axis=1).astype(BF16)
        early = (
            gram_of(0, panel[quad, dirs : 2 * dirs])
            + gram_of(chunks, packed)
            + gram_of(1, panel[quad, :dirs])
        )
        arrival(tail, brecv, t)
        cpart, hpart = halves_of(early + gram_of(2, tail[quad]))
        for i, both in enumerate(
            (
                jnp.where(low, cpart, pltpu.roll(hpart, CHUNK, 1)),
                jnp.where(low, pltpu.roll(cpart, CHUNK, 1), hpart),
            )
        ):
            to = 2 * t + i
            hi, lo = two_terms(both[dirs:] + small)
            msg[to] = jnp.concatenate([both[:dirs], hi, lo], axis=0).astype(BF16)

            @pl.when(to != w)
            def _():
                pltpu.make_async_remote_copy(
                    src_ref=msg.at[to], dst_ref=got.at[w], send_sem=msend, recv_sem=mrecv,
                    device_id=(to, b), device_id_type=MESH,
                ).start()

    got[w] = msg[w]

    others = pl.ds(0, nb - 1)
    for part, sem in ((panel.at[others, dirs:], asend), (panel.at[others, :dirs], csend)):
        pltpu.make_async_copy(part, part, sem).wait()
    pltpu.make_async_copy(tail.at[others], tail.at[others], bsend).wait()
    groups = pl.ds(0, nw - 1)
    pltpu.make_async_copy(got.at[groups], got.at[groups], mrecv).wait()

    total = jnp.zeros((dirs, LANES), F32)
    for i in range(nw):
        one = got[i].astype(F32)
        total = total + one[:dirs]
        vecs[i] = one[dirs : dirs + 8] + one[dirs + 8 :]
    jsum, jshift = vecs[:, 0], vecs[:, 1]
    isum, usum, ishift = vecs[:, 2, :dirs], vecs[:, 3, :dirs], vecs[:, 4, :dirs]
    esum, live = vecs[:, 5], vecs[:, 6]
    inv = 1.0 / jnp.sum(live, axis=0, keepdims=True)
    jref = jnp.sum(jnp.where(low, jsum, 0.0) + live * jshift, axis=0, keepdims=True) * inv
    iref = (
        jnp.sum(isum + live[:, :dirs] * ishift, axis=0, keepdims=True) * inv[:, :dirs]
    )
    jdiff = jshift - jref
    pdiff = jnp.where(low, 0.0, pltpu.roll(jdiff, CHUNK, 1))
    left = jnp.concatenate([usum, isum, ishift - iref], axis=0)
    right = jnp.concatenate([pdiff, jdiff, jsum + live * jdiff + esum * pdiff], axis=0)
    o_ref[...] = (total + exact_dot(left, right, TN)) * inv
    pltpu.make_async_copy(got.at[groups], got.at[groups], msend).wait()


def solution(mesh):
    nw, nb = mesh.shape["walk"], mesh.shape["blk"]

    def per_device(derivs, energy_grads, local_energy, directions, widths, live_rows):
        rows, cols = derivs.shape
        dirs = directions.shape[0]
        chunks = rows // CHUNK
        hbm_spec = pl.BlockSpec(memory_space=pltpu.HBM)
        smem_spec = pl.BlockSpec(memory_space=pltpu.SMEM)
        dma = pltpu.SemaphoreType.DMA
        out = pl.pallas_call(
            functools.partial(pencil_kernel, nw, nb),
            out_shape=jax.ShapeDtypeStruct((dirs, LANES), F32),
            in_specs=[hbm_spec] * 4 + [smem_spec] * 2,
            out_specs=pl.BlockSpec(memory_space=pltpu.VMEM),
            scratch_shapes=[
                pltpu.VMEM((rows, cols), BF16),
                pltpu.VMEM((rows, cols), BF16),
                pltpu.VMEM((dirs, cols), BF16),
                pltpu.VMEM((1, rows), F32),
                pltpu.VMEM((nb, 2 * dirs + dirs // 2, LANES), BF16),
                pltpu.VMEM((nb, dirs, LANES), BF16),
                pltpu.VMEM((chunks + 1, 4 * dirs + 16, LANES), BF16),
                pltpu.VMEM((nw, dirs + 16, LANES), BF16),
                pltpu.VMEM((nw, dirs + 16, LANES), BF16),
                pltpu.VMEM((nw, 8, LANES), F32),
                dma((chunks * SPLIT,)),
                dma((chunks * SPLIT,)),
                dma((2 * SPLIT,)),
                dma((nb // 4,)),
                dma((nb // 4,)),
            ]
            + [dma(())] * 6,
            compiler_params=pltpu.CompilerParams(
                collective_id=0, has_side_effects=True, vmem_limit_bytes=53 << 20
            ),
            name="pencil",
        )(
            derivs, energy_grads, directions,
            pltpu.with_memory_space_constraint(local_energy.reshape(1, rows), pltpu.HBM),
            widths, live_rows,
        )
        return out[:, CHUNK:], out[:, :CHUNK]

    return jax.shard_map(
        per_device,
        mesh=mesh,
        in_specs=(
            P("walk", "blk"), P("walk", "blk"), P("walk"), P("blk", None), P("blk"), P("walk"),
        ),
        out_specs=(P("blk", "walk"), P("blk", "walk")),
        check_vma=False,
    )
```
